32 devices in a mesh: gz: 4 (over y, x), gy: 2 (over core), gx: 4 (over z).
Axes of the slice: x: 2, y: 2, z: 4, core: 2. Of those that a mesh axis runs over, the one named last changes fastest.
Arguments:
- populations: float32 [19, 32, 16, 512], P(None, 'gz', 'gy', 'gx'), may hold values from 0.1 to 20, as said below
- solid: int32 [32, 16, 512], P('gz', 'gy', 'gx'), may hold values 0 or 1
- ports: int32 [2, 16, 512], P(None, 'gy', 'gx'), may hold values 0 or 1
- concentration: float32 [2, 4, 2, 64], P(None, 'gz'), may hold values from 0 to 1
- loaded: float32 [2, 4, 2, 64], P(None, 'gz'), may hold values from 0 to 2
Outputs:
- final_populations: float32 [19, 32, 16, 512], P(None, 'gz', 'gy', 'gx')
- new_concentration: float32 [2, 4, 2, 64], P(None, 'gz')
- new_loaded: float32 [2, 4, 2, 64], P(None, 'gz')
The draws below stay inside these ranges and needn't reach their ends.
Inputs may be any that keep to these rules, and one draw needn't show every extreme that they name: `populations`: every population is positive and of the size of its lattice weight times 36.
All inputs are finite; a program needn't handle non-finite values. No bound on the sum of `solid` or of `ports` on one device may be relied on, other than what follows from the above.
Results may differ from the reference program's by a relative error of at most 0.00002.
Values sent between devices are 32-bit elements; how exact they have to be, the bound alone decides.
A program may use at most 64 MiB of HBM per device.

```python
import jax
import jax.numpy as jnp

ITERS = 2
NZ = 32
NY = 16
NX = 512
NCZ = 4
NCY = 2
NCX = 64


lattice = [(0, 0, 0), (1, 0, 0), (-1, 0, 0), (0, 1, 0), (0, -1, 0), (0, 0, 1), (0, 0, -1), (1, 1, 0), (-1, -1, 0), (1, -1, 0), (-1, 1, 0), (1, 0, 1), (-1, 0, -1), (1, 0, -1), (-1, 0, 1), (0, 1, 1), (0, -1, -1), (0, 1, -1), (0, -1, 1)]


weights = [1.0 / 3.0] + [1.0 / 18.0] * 6 + [1.0 / 36.0] * 12


def draw_populations(key, part):
    keys = jax.random.split(key, 5)
    grid = (NZ, NY, NX)
    density = 36.0 * jax.random.uniform(keys[0], grid, jnp.float32, 0.9, 1.1)
    speed_z = jax.random.uniform(keys[1], grid, jnp.float32, 0.02, 0.1)
    noise = jax.random.uniform(keys[4], (19,) + grid, jnp.float32, -0.3, 0.3)
    speed_y = jax.random.uniform(keys[2], grid, jnp.float32, -0.02, 0.02)
    speed_x = jax.random.uniform(keys[3], grid, jnp.float32, -0.02, 0.02)
    square = speed_z * speed_z + speed_y * speed_y + speed_x * speed_x
    result = []
    for member in range(19):
        step_z, step_y, step_x = lattice[member]
        along = step_z * speed_z + step_y * speed_y + step_x * speed_x
        result.append(weights[member] * density * (1.0 + 3.0 * along + 4.5 * along * along - 1.5 * square))
    return jnp.stack(result) * (1.0 + noise)


def set_ends(values, rng, least, largest):
    longest = values.shape.index(max(values.shape))
    spots = []
    for shift in (0, 1):
        where = [jax.random.randint(jax.random.fold_in(rng, axis), (), 0, length) for axis, length in enumerate(values.shape)]
        where[longest] = (where[longest] + shift) % values.shape[longest]
        spots.append(tuple(where))
    return values.at[spots[0]].set(least).at[spots[1]].set(largest)


def levels(stream_key, shape, cuts, smallest, largest):
    gain, own = 1.0, jax.random.fold_in(stream_key, 6)
    for axis_at, blocks in cuts:
        draws = jnp.exp(jax.random.uniform(jax.random.fold_in(own, axis_at), (blocks,), jnp.float32, smallest / len(cuts), largest / len(cuts)))
        gain = gain * jnp.repeat(draws, shape[axis_at] // blocks).reshape([-1 if axis == axis_at else 1 for axis in range(len(shape))])
    return gain


def setup_inputs(seed: int = 0) -> dict:
    key_list = jax.random.split(jax.random.key(seed), 6)
    return {
        "populations": draw_populations(jax.random.fold_in(key_list[5], 71), 0),
        "solid": set_ends((jax.random.randint(key_list[1], (NZ, NY, NX), 0, 5) < 2).astype(jnp.int32), jax.random.fold_in(key_list[1], 1), 0, 1),
        "ports": set_ends((jax.random.randint(key_list[2], (2, NY, NX), 0, 4) < 3).astype(jnp.int32), jax.random.fold_in(key_list[2], 1), 0, 1),
        "concentration": jnp.clip(1.0 * jax.random.uniform(key_list[3], (2, NCZ, NCY, NCX), jnp.float32) ** levels(key_list[3], (2, NCZ, NCY, NCX), ((1, 4),), -0.2, 0.2), 0.0, 1.0),
        "loaded": jnp.clip(2.0 * jax.random.uniform(key_list[4], (2, NCZ, NCY, NCX), jnp.float32) ** levels(key_list[4], (2, NCZ, NCY, NCX), ((1, 4),), -0.2, 0.2), 0.0, 2.0),
    }


lattice = [(0, 0, 0), (1, 0, 0), (-1, 0, 0), (0, 1, 0), (0, -1, 0), (0, 0, 1), (0, 0, -1),
           (1, 1, 0), (-1, -1, 0), (1, -1, 0), (-1, 1, 0), (1, 0, 1), (-1, 0, -1), (1, 0, -1), (-1, 0, 1),
           (0, 1, 1), (0, -1, -1), (0, 1, -1), (0, -1, 1)]
opposite = [0, 2, 1, 4, 3, 6, 5, 8, 7, 10, 9, 12, 11, 14, 13, 16, 15, 18, 17]
weights = [1.0 / 3.0] + [1.0 / 18.0] * 6 + [1.0 / 36.0] * 12
relax_rate = 1.25
base_density = 36.0
inlet_speed = 0.05
spread_base = (0.03, 0.06)
spread_length = 0.1
uptake_rate = (0.3, 0.6)
affinity = (2.0, 0.5)
phase_ratio = 0.5
feed_level = (1.0, 0.5)


def equilibrium(density, velocity):
    speed_z, speed_y, speed_x = velocity
    square = speed_z * speed_z + speed_y * speed_y + speed_x * speed_x
    result = []
    for member in range(19):
        step_z, step_y, step_x = lattice[member]
        along = step_z * speed_z + step_y * speed_y + step_x * speed_x
        result.append(weights[member] * density * (1.0 + 3.0 * along + 4.5 * along * along - 1.5 * square))
    return result


def moments(pops):
    density = pops[0]
    for member in range(1, 19):
        density = density + pops[member]
    flows = []
    for position in range(3):
        total = jnp.zeros_like(pops[0])
        for member in range(19):
            heading = lattice[member][position]
            if heading == 1:
                total = total + pops[member]
            elif heading == -1:
                total = total - pops[member]
        flows.append(total)
    return density, flows


def collide(pops, solid_flag):
    density, flows = moments(pops)
    velocity = [flow / density for flow in flows]
    balance = equilibrium(density, velocity)
    post = [jnp.where(solid_flag, pops[opposite[member]],
                      pops[member] - relax_rate * (pops[member] - balance[member])) for member in range(19)]
    return post, velocity


def close_ends(moved, post, velocity, ports, first_dev, last_dev):
    inflow = equilibrium(base_density, (inlet_speed, 0.0, 0.0))
    outflow = equilibrium(base_density, (velocity[0][-1], velocity[1][-1], velocity[2][-1]))
    inlet_open = ports[0] == 1
    outlet_open = ports[1] == 1
    result = list(moved)
    for member in range(19):
        step_z = lattice[member][0]
        back = post[opposite[member]]
        if step_z == 1:
            entering = jnp.where(inlet_open, inflow[member], back[0])
            result[member] = result[member].at[0].set(jnp.where(first_dev, entering, result[member][0]))
        elif step_z == -1:
            entering = jnp.where(outlet_open, outflow[member], back[-1])
            result[member] = result[member].at[-1].set(jnp.where(last_dev, entering, result[member][-1]))
    return result


def block_sum(field):
    depth, height, width = field.shape
    return field.reshape(depth // 8, 8, height // 8, 8, width // 8, 8).sum(axis=(1, 3, 5))


def cell_velocity(pops, solid):
    density, flows = moments(pops)
    fluid = (solid == 0).astype(pops[0].dtype)
    return jnp.stack([block_sum(flow * fluid) for flow in flows]) / (512.0 * base_density)


def transport(padded, loaded, coarse_vel):
    centre = padded[:, 1:-1]
    neighbours = [(padded[:, :-2], padded[:, 2:]),
                  (jnp.roll(centre, 1, axis=2), jnp.roll(centre, -1, axis=2)),
                  (jnp.roll(centre, 1, axis=3), jnp.roll(centre, -1, axis=3))]
    change = jnp.zeros_like(centre)
    curvature = jnp.zeros_like(centre)
    reach = jnp.zeros_like(coarse_vel[0])
    for direction in range(3):
        courant = 8.0 * coarse_vel[direction]
        before, after = neighbours[direction]
        change = change - jnp.maximum(courant, 0.0) * (centre - before) - jnp.minimum(courant, 0.0) * (after - centre)
        curvature = curvature + after - 2.0 * centre + before
        reach = reach + jnp.abs(courant)
    base = jnp.array(spread_base, dtype=centre.dtype)[:, None, None, None]
    speed = jnp.array(uptake_rate, dtype=centre.dtype)[:, None, None, None]
    holding = jnp.array(affinity, dtype=centre.dtype)[:, None, None, None]
    rate = speed * (holding * centre - loaded)
    new_conc = centre + change + (base + spread_length * reach) * curvature - phase_ratio * rate
    return new_conc, loaded + rate


def reference(populations, solid, ports, concentration, loaded):
    pops = [populations[member] for member in range(19)]
    solid_flag = solid == 1
    for iteration in range(ITERS):
        post, velocity = collide(pops, solid_flag)
        moved = []
        for member in range(19):
            step_z, step_y, step_x = lattice[member]
            moved.append(jnp.roll(post[member], (step_z, step_y, step_x), axis=(0, 1, 2)))
        pops = close_ends(moved, post, velocity, ports, True, True)
    final = jnp.stack(pops)
    coarse_vel = cell_velocity(pops, solid)
    feed = jnp.broadcast_to(jnp.array(feed_level, dtype=concentration.dtype)[:, None, None],
                            (2, concentration.shape[2], concentration.shape[3]))
    padded = jnp.concatenate([feed[:, None], concentration, concentration[:, -1:]], axis=1)
    new_conc, new_load = transport(padded, loaded, coarse_vel)
    return (final, new_conc, new_load)
```

```python
import functools

import jax
import jax.numpy as jnp
from jax import lax
from jax.experimental import pallas as pl
from jax.experimental.pallas import tpu as pltpu
from jax.sharding import PartitionSpec as P

ITERS = 2
CELL = 8
MESH = pl.DeviceIdType.MESH

lattice = [
    (0, 0, 0),
    (1, 0, 0),
    (-1, 0, 0),
    (0, 1, 0),
    (0, -1, 0),
    (0, 0, 1),
    (0, 0, -1),
    (1, 1, 0),
    (-1, -1, 0),
    (1, -1, 0),
    (-1, 1, 0),
    (1, 0, 1),
    (-1, 0, -1),
    (1, 0, -1),
    (-1, 0, 1),
    (0, 1, 1),
    (0, -1, -1),
    (0, 1, -1),
    (0, -1, 1),
]
opposite = [0, 2, 1, 4, 3, 6, 5, 8, 7, 10, 9, 12, 11, 14, 13, 16, 15, 18, 17]
weights = [1.0 / 3.0] + [1.0 / 18.0] * 6 + [1.0 / 36.0] * 12
relax_rate = 1.25
base_density = 36.0
inlet_speed = 0.05
spread_base = (0.03, 0.06)
spread_length = 0.1
uptake_rate = (0.3, 0.6)
affinity = (2.0, 0.5)
phase_ratio = 0.5
feed_level = (1.0, 0.5)

GROUPS = [[[m for m in range(19) if lattice[m][d] == s] for s in (1, -1)] for d in range(3)]
ORDER = GROUPS[0][0] + GROUPS[0][1] + [m for m in range(19) if lattice[m][0] == 0]
SLOT = {m: i for i, m in enumerate(ORDER)}
ZY, ZX, YX = (7, 8, 9, 10), (11, 12, 13, 14), (15, 16, 17, 18)


def side(step):
    return 0 if step == 1 else 1


def moments(f):
    density = f[0]
    for member in range(1, 19):
        density = density + f[member]
    return density, momentum(f)


def momentum(f):
    flows = []
    for d in range(3):
        total = None
        for a, b in zip(GROUPS[d][0], [opposite[m] for m in GROUPS[d][0]]):
            part = f[a] - f[b]
            total = part if total is None else total + part
        flows.append(total)
    return flows


def balance(scale, velocity, members):
    square = velocity[0] * velocity[0] + velocity[1] * velocity[1] + velocity[2] * velocity[2]
    base = 1.0 - 1.5 * square
    cache, result = {}, {}
    for w in set(weights[m] for m in members):
        cache[w] = scale * w
    for m in members:
        if m == 0:
            result[m] = cache[weights[0]] * base
            continue
        key = min(m, opposite[m])
        if ("pair", key) not in cache:
            along = None
            for d in range(3):
                step = lattice[key][d]
                if step:
                    term = velocity[d]
                    if along is None:
                        along = term if step == 1 else -term
                    else:
                        along = along + term if step == 1 else along - term
            cache[("pair", key)] = (base + 4.5 * along * along, 3.0 * along)
        even, odd = cache[("pair", key)]
        result[m] = cache[weights[m]] * (even + odd if m == key else even - odd)
    return result


def collide(f, solid):
    density, flows = moments(f)
    inverse = 1.0 / density
    velocity = [flow * inverse for flow in flows]
    feq = balance(relax_rate * density, velocity, range(19))
    post = [
        jnp.where(solid, f[opposite[m]], (1.0 - relax_rate) * f[m] + feq[m]) for m in range(19)
    ]
    return post, velocity


def kernel(sizes, *refs):
    nz, ny, nx = sizes
    (pop_hbm, solid_hbm, ports_hbm, conc_hbm, load_hbm, out, new_conc, new_load,
     pops, solid, ports, conc, load, post0, post1, speed, ypack, xpack,
     zrecv, yrecv, xrecv, zyrecv, zxrecv, yxrecv, corner, near, wrapped,
     sent_v, all_v, vel, load_sem, send_sem, recv_sem, near_sem, vsend, vrecv) = refs
    D, H, W = solid.shape
    ncy, ncx = conc.shape[2:]
    gz, gy, gx = lax.axis_index("gz"), lax.axis_index("gy"), lax.axis_index("gx")
    is_first, is_last = gz == 0, gz == nz - 1
    has_up, has_down = gz < nz - 1, gz > 0

    small = [
        pltpu.make_async_copy(a, b, load_sem.at[D + i])
        for i, (a, b) in enumerate(
            ((solid_hbm, solid), (ports_hbm, ports), (conc_hbm, conc), (load_hbm, load)))
    ]
    small[0].start()

    def plane_in(z):
        return pltpu.make_async_copy(pop_hbm.at[:, z], pops.at[:, z], load_sem.at[z])

    for z in range(D):
        plane_in(z).start()
    for copy in small[1:]:
        copy.start()

    def at(offset):
        dz, dy, dx = offset
        return {"gz": gz + dz, "gy": lax.rem(gy + dy + ny, ny), "gx": lax.rem(gx + dx + nx, nx)}

    flat = [(0, dy, dx) for dy in range(ny) for dx in range(nx) if dy or dx]
    cross = sorted({(dy % ny, dx % nx) for dy, dx in ((0, 0), (1, 0), (-1, 0), (0, 1), (0, -1))})
    barrier = pltpu.get_barrier_semaphore()

    def greet(offsets):
        for offset in offsets:
            pl.semaphore_signal(barrier, inc=1, device_id=at(offset), device_id_type=MESH)

    greet(flat)

    @pl.when(has_up)
    def _():
        greet([(1, dy, dx) for dy, dx in cross])

    @pl.when(has_down)
    def _():
        greet([(-1, dy, dx) for dy, dx in cross])

    lane = lax.broadcasted_iota(jnp.int32, (H, W), 1)
    row = lax.broadcasted_iota(jnp.int32, (H, W), 0)
    edge_lane = [lane == 0, lane == W - 1]
    edge_row = [row == 0, row == H - 1]
    first_mask = jnp.full((H, W), gz, jnp.int32) == 0
    last_mask = jnp.full((H, W), gz, jnp.int32) == nz - 1

    def rolled(x, step, axis):
        size = x.shape[axis]
        return pltpu.roll(x, step % size, axis)

    def blank(s):
        for it in range(ITERS):
            zrecv[it, s] = jnp.zeros(zrecv.shape[2:], jnp.float32)
            for at_member in range(4):
                if side(lattice[ZY[at_member]][0]) == s:
                    zyrecv[it, at_member] = jnp.zeros((H, W), jnp.float32)
                if side(lattice[ZX[at_member]][0]) == s:
                    zxrecv[it, at_member] = jnp.zeros((H, W), jnp.float32)

    for i in range(4):
        if i != 0:
            small[i].wait()

    @pl.when(is_first)
    def _():
        blank(0)
        for s in range(2):
            near[0, s] = jnp.full(near.shape[2:], feed_level[s], jnp.float32)

    @pl.when(is_last)
    def _():
        blank(1)
        near[1] = conc[...]

    posts = (post0, post1)

    def store_post(it, z, post, packs):
        where = posts[it]
        for m in range(19):
            where[SLOT[m], z] = post[m]
        for s in range(2):
            for i, m in enumerate(GROUPS[1][s]):
                edge = post[m][H - 1 :, :] if s == 0 else post[m][:1, :]
                ypack[it, s, i, pl.ds(z, 1), :] = edge
        new = []
        for s in range(2):
            acc = packs[s]
            for i, m in enumerate(GROUPS[2][s]):
                k = i * D + z
                acc = jnp.where(lane == k, pltpu.roll(post[m], k + 1 - s, 1), acc)
            new.append(acc)
        return tuple(new)

    def finish(it, packs):
        for s in range(2):
            xpack[it, s] = packs[s]

    def exchange(it):
        where = posts[it]
        moves = []
        for m in ZX:
            z = D - 1 if lattice[m][0] == 1 else 0
            moves.append((where.at[SLOT[m], z], zxrecv.at[it, m - ZX[0]], lattice[m]))
        for s in range(2):
            moves.append((xpack.at[it, s], xrecv.at[it, s], (0, 0, 1 - 2 * s)))
        for m in YX:
            s = side(lattice[m][1])
            moves.append((ypack.at[it, s, GROUPS[1][s].index(m)], yxrecv.at[it, m - YX[0]], lattice[m]))
        for m in ZY:
            z = D - 1 if lattice[m][0] == 1 else 0
            moves.append((where.at[SLOT[m], z], zyrecv.at[it, m - ZY[0]], lattice[m]))
        for s in range(2):
            z = D - 1 if s == 0 else 0
            moves.append((where.at[pl.ds(5 * s, 5), z], zrecv.at[it, s], (1 - 2 * s, 0, 0)))
        for s in range(2):
            moves.append((ypack.at[it, s], yrecv.at[it, s], (0, 1 - 2 * s, 0)))
        copies = {-1: [], 0: [], 1: []}
        for i, (src, dst, offset) in enumerate(moves):
            copies[offset[0]].append(
                pltpu.make_async_remote_copy(
                    src_ref=src, dst_ref=dst, send_sem=send_sem.at[it, i],
                    recv_sem=recv_sem.at[it, i], device_id=at(offset), device_id_type=MESH))
        return copies

    def run(copies, method, incoming=False):
        conds = {1: has_down, -1: has_up} if incoming else {1: has_up, -1: has_down}
        for dz in (1, -1):
            @pl.when(conds[dz])
            def _():
                for copy in copies[dz]:
                    getattr(copy, method)()
        for copy in copies[0]:
            getattr(copy, method)()

    small[0].wait()
    zero = jnp.zeros((H, W), jnp.float32)

    def first_plane(z, packs):
        plane_in(z).wait()
        f = [pops[m, z] for m in range(19)]
        post, velocity = collide(f, solid[z] == 1)
        if isinstance(z, int):
            for d in range(3):
                speed[0, d] = velocity[d]
        return store_post(0, z, post, packs)

    packs = lax.fori_loop(0, D - 1, first_plane, (zero, zero))
    packs = first_plane(D - 1, packs)
    finish(0, packs)

    up_down = jnp.where(has_up, len(cross), 0) + jnp.where(has_down, len(cross), 0)
    pl.semaphore_wait(barrier, len(flat) + up_down)

    moves0 = exchange(0)
    run(moves0, "start")
    ends = {1: [], -1: [], 0: []}
    for s in range(2):
        dz = 1 - 2 * s
        ends[dz].append(
            pltpu.make_async_remote_copy(
                src_ref=conc, dst_ref=near.at[s], send_sem=near_sem.at[0, s],
                recv_sem=near_sem.at[1, s], device_id=at((dz, 0, 0)), device_id_type=MESH))
    run(ends, "start")

    def arrive(it, copies):
        run(copies, "wait_recv", incoming=True)
        for m in YX:
            _, cy, cx = lattice[m]
            s = side(cy)
            own = rolled(yrecv[it, s, GROUPS[1][s].index(m)], cx, 1)
            far = rolled(yxrecv[it, m - YX[0]], cx, 1)
            corner[it, m - YX[0]] = jnp.where(edge_lane[side(cx)], far, own)

    def stream(it, z, place):
        where = posts[it]
        f = []
        for m in range(19):
            cz, cy, cx = lattice[m]
            beyond = (cz == 1 and place == "low") or (cz == -1 and place == "high")
            if beyond:
                s = side(cz)
                v = zrecv[it, s, GROUPS[0][s].index(m)]
            else:
                v = where[SLOT[m], z - cz]
            if cx:
                s = side(cx)
                if beyond:
                    column = rolled(zxrecv[it, m - ZX[0]], cx, 1)
                else:
                    k = GROUPS[2][s].index(m) * D + z - cz
                    column = pltpu.roll(xrecv[it, s], W - k if s == 0 else W - 1 - k, 1) \
                        if not (isinstance(k, int) and k == 0 and s == 0) else xrecv[it, s]
                v = jnp.where(edge_lane[s], column, rolled(v, cx, 1))
            if cy:
                s = side(cy)
                if beyond:
                    r = H - 1 if s == 0 else 0
                    line = zyrecv[it, m - ZY[0], r : r + 1, :]
                elif cx:
                    line = corner[it, m - YX[0], pl.ds(z, 1), :]
                else:
                    line = yrecv[it, s, GROUPS[1][s].index(m), pl.ds(z - cz, 1), :]
                v = jnp.where(edge_row[s], jnp.broadcast_to(line, (H, W)), rolled(v, cy, 0))
            f.append(v)
        if place == "low":
            inflow = equilibrium_at_inlet()
            opened = ports[0] == 1
            for m in GROUPS[0][0]:
                back = where[SLOT[opposite[m]], 0]
                f[m] = jnp.where(first_mask, jnp.where(opened, inflow[m], back), f[m])
        if place == "high":
            velocity = [speed[it, d] for d in range(3)]
            outflow = balance(base_density, velocity, GROUPS[0][1])
            opened = ports[1] == 1
            for m in GROUPS[0][1]:
                back = where[SLOT[opposite[m]], D - 1]
                f[m] = jnp.where(last_mask, jnp.where(opened, outflow[m], back), f[m])
        return f

    def planes(step, carry):
        carry = step(0, "low", carry)
        carry = lax.fori_loop(1, D - 1, lambda z, c: step(z, "mid", c), carry)
        return step(D - 1, "high", carry)

    arrive(0, moves0)

    def second_plane(z, place, packs):
        f = stream(0, z, place)
        post, velocity = collide(f, solid[z] == 1)
        if place == "high":
            for d in range(3):
                speed[1, d] = velocity[d]
        return store_post(1, z, post, packs)

    finish(1, planes(second_plane, (zero, zero)))
    moves1 = exchange(1)
    run(moves1, "start")

    run(ends, "wait_recv", incoming=True)
    source = lax.broadcasted_iota(jnp.int32, (ncx, ncx), 0)
    target = lax.broadcasted_iota(jnp.int32, (ncx, ncx), 1)
    ahead = jnp.where(target == ncx - 1, 0, target + 1)
    behind = jnp.where(target == 0, ncx - 1, target - 1)
    take_after = (source == ahead).astype(jnp.float32)
    take_before = (source == behind).astype(jnp.float32)

    def exact_dot(a, b):
        return jnp.dot(a, b, precision=lax.Precision.HIGHEST, preferred_element_type=jnp.float32)

    diffs = []
    for s in range(2):
        c = conc[s, 0]
        wrapped[s, 1 : ncy + 1, :] = c
        wrapped[s, 0:1, :] = conc[s, 0, ncy - 1 : ncy, :]
        wrapped[s, ncy + 1 : ncy + 2, :] = conc[s, 0, 0:1, :]
        pairs = [
            (near[0, s, 0], near[1, s, 0]),
            (wrapped[s, 0:ncy, :], wrapped[s, 2 : ncy + 2, :]),
            (exact_dot(c, take_before), exact_dot(c, take_after)),
        ]
        curvature = sum(b + a - 2.0 * c for b, a in pairs)
        rate = uptake_rate[s] * (affinity[s] * c - load[s, 0])
        new_load[s, 0] = load[s, 0] + rate
        diffs.append((c - phase_ratio * rate + spread_base[s] * curvature, curvature,
                      [(c - b, a - c) for b, a in pairs]))

    arrive(1, moves1)

    def last_plane(z, place, totals):
        f = stream(1, z, place)
        for m in range(19):
            out[m, z] = f[m]
        pore = solid[z] == 0
        return tuple(t + jnp.where(pore, flow, 0.0) for t, flow in zip(totals, momentum(f)))

    totals = planes(last_plane, (zero, zero, zero))
    sums = zero
    for d in range(3):
        line = jnp.sum(totals[d], axis=0, keepdims=True)
        sums = jnp.where(row == d, jnp.broadcast_to(line, (H, W)), sums)
    wide = sent_v.shape[1]
    voxel = lax.broadcasted_iota(jnp.int32, (W, wide), 0)
    cell = lax.broadcasted_iota(jnp.int32, (W, wide), 1) - gx * (W // CELL)
    pick = ((voxel >= cell * CELL) & (voxel < cell * CELL + CELL)).astype(jnp.float32)
    sent_v[...] = exact_dot(sums, pick) * (1.0 / (CELL * CELL * CELL * base_density))
    tell = [
        pltpu.make_async_remote_copy(
            src_ref=sent_v, dst_ref=all_v.at[gy, gx], send_sem=vsend.at[i],
            recv_sem=vrecv.at[i], device_id=at(offset), device_id_type=MESH)
        for i, offset in enumerate(flat)
    ]
    for copy in tell:
        copy.start()
    all_v[gy, gx] = sent_v[...]
    run(moves0, "wait_send")
    run(moves1, "wait_send")
    run(ends, "wait_send")
    for copy in tell:
        copy.wait_recv()

    for y in range(ny):
        total = all_v[y, 0]
        for x in range(1, nx):
            total = total + all_v[y, x]
        for d in range(3):
            vel[d, y : y + 1, :] = total[d : d + 1, :]
    courant = [CELL * vel[d][:, :ncx] for d in range(3)]
    reach = jnp.abs(courant[0]) + jnp.abs(courant[1]) + jnp.abs(courant[2])
    for s in range(2):
        value, curvature, steps = diffs[s]
        for d in range(3):
            low, high = steps[d]
            value = value - jnp.maximum(courant[d], 0.0) * low - jnp.minimum(courant[d], 0.0) * high
        new_conc[s, 0] = value + spread_length * reach * curvature
    for copy in tell:
        copy.wait_send()


def equilibrium_at_inlet():
    result = {}
    for m in GROUPS[0][0]:
        along = inlet_speed
        result[m] = weights[m] * base_density * (
            1.0 + 3.0 * along + 4.5 * along * along - 1.5 * inlet_speed * inlet_speed)
    return result


def solution(mesh):
    sizes = tuple(mesh.shape[a] for a in ("gz", "gy", "gx"))
    nz, ny, nx = sizes

    def body(populations, solid, ports, concentration, loaded):
        D, H, W = solid.shape
        ncy, ncx = concentration.shape[2:]
        assert D == CELL and H == CELL and W % 128 == 0 and 5 * D <= W
        wide = -(-ncx // 128) * 128
        f32 = jnp.float32
        tile = (H, W)
        anywhere = pl.BlockSpec(memory_space=pl.ANY)
        inside = pl.BlockSpec(memory_space=pltpu.VMEM)
        return pl.pallas_call(
            functools.partial(kernel, sizes),
            out_shape=(
                jax.ShapeDtypeStruct(populations.shape, f32),
                jax.ShapeDtypeStruct(concentration.shape, f32),
                jax.ShapeDtypeStruct(loaded.shape, f32),
            ),
            in_specs=[anywhere] * 5,
            out_specs=(inside,) * 3,
            scratch_shapes=[
                pltpu.VMEM(populations.shape, f32),
                pltpu.VMEM(solid.shape, jnp.int32),
                pltpu.VMEM(ports.shape, jnp.int32),
                pltpu.VMEM(concentration.shape, f32),
                pltpu.VMEM(loaded.shape, f32),
                pltpu.VMEM((19, D) + tile, f32),
                pltpu.VMEM((19, D) + tile, f32),
                pltpu.VMEM((ITERS, 3) + tile, f32),
                pltpu.VMEM((ITERS, 2, 5, D, W), f32),
                pltpu.VMEM((ITERS, 2) + tile, f32),
                pltpu.VMEM((ITERS, 2, 5) + tile, f32),
                pltpu.VMEM((ITERS, 2, 5, D, W), f32),
                pltpu.VMEM((ITERS, 2) + tile, f32),
                pltpu.VMEM((ITERS, 4) + tile, f32),
                pltpu.VMEM((ITERS, 4) + tile, f32),
                pltpu.VMEM((ITERS, 4, D, W), f32),
                pltpu.VMEM((ITERS, 4, D, W), f32),
                pltpu.VMEM((2,) + concentration.shape, f32),
                pltpu.VMEM((2, ncy + 2, ncx), f32),
                pltpu.VMEM((8, wide), f32),
                pltpu.VMEM((ny, nx, 8, wide), f32),
                pltpu.VMEM((3, ncy, wide), f32),
                pltpu.SemaphoreType.DMA((D + 4,)),
                pltpu.SemaphoreType.DMA((ITERS, 18)),
                pltpu.SemaphoreType.DMA((ITERS, 18)),
                pltpu.SemaphoreType.DMA((2, 2)),
                pltpu.SemaphoreType.DMA((ny * nx - 1,)),
                pltpu.SemaphoreType.DMA((ny * nx - 1,)),
            ],
            compiler_params=pltpu.CompilerParams(collective_id=0, has_side_effects=True),
        )(populations, solid, ports, concentration, loaded)

    placed = (
        P(None, "gz", "gy", "gx"),
        P("gz", "gy", "gx"),
        P(None, "gy", "gx"),
        P(None, "gz", None, None),
        P(None, "gz", None, None),
    )
    return jax.shard_map(
        body,
        mesh=mesh,
        in_specs=placed,
        out_specs=(P(None, "gz", "gy", "gx"), P(None, "gz", None, None), P(None, "gz", None, None)),
        check_vma=False,
    )
```

```python
import functools

import jax
import jax.numpy as jnp
from jax import lax
from jax.experimental import pallas as pl
from jax.experimental.pallas import tpu as pltpu
from jax.sharding import PartitionSpec as P

ITERS = 2
CELL = 8
MESH = pl.DeviceIdType.MESH

lattice = [
    (0, 0, 0),
    (1, 0, 0),
    (-1, 0, 0),
    (0, 1, 0),
    (0, -1, 0),
    (0, 0, 1),
    (0, 0, -1),
    (1, 1, 0),
    (-1, -1, 0),
    (1, -1, 0),
    (-1, 1, 0),
    (1, 0, 1),
    (-1, 0, -1),
    (1, 0, -1),
    (-1, 0, 1),
    (0, 1, 1),
    (0, -1, -1),
    (0, 1, -1),
    (0, -1, 1),
]
opposite = [0, 2, 1, 4, 3, 6, 5, 8, 7, 10, 9, 12, 11, 14, 13, 16, 15, 18, 17]
weights = [1.0 / 3.0] + [1.0 / 18.0] * 6 + [1.0 / 36.0] * 12
relax_rate = 1.25
base_density = 36.0
inlet_speed = 0.05
spread_base = (0.03, 0.06)
spread_length = 0.1
uptake_rate = (0.3, 0.6)
affinity = (2.0, 0.5)
phase_ratio = 0.5
feed_level = (1.0, 0.5)

GROUPS = [[[m for m in range(19) if lattice[m][d] == s] for s in (1, -1)] for d in range(3)]
ORDER = GROUPS[0][0] + GROUPS[0][1] + [m for m in range(19) if lattice[m][0] == 0]
SLOT = {m: i for i, m in enumerate(ORDER)}
ZY, ZX, YX = (7, 8, 9, 10), (11, 12, 13, 14), (15, 16, 17, 18)


def side(step):
    return 0 if step == 1 else 1


def moments(f):
    density = f[0]
    for member in range(1, 19):
        density = density + f[member]
    return density, momentum(f)


def momentum(f):
    flows = []
    for d in range(3):
        total = None
        for a, b in zip(GROUPS[d][0], [opposite[m] for m in GROUPS[d][0]]):
            part = f[a] - f[b]
            total = part if total is None else total + part
        flows.append(total)
    return flows


def balance(scale, velocity, members):
    square = velocity[0] * velocity[0] + velocity[1] * velocity[1] + velocity[2] * velocity[2]
    base = 1.0 - 1.5 * square
    cache, result = {}, {}
    for w in set(weights[m] for m in members):
        cache[w] = scale * w
    for m in members:
        if m == 0:
            result[m] = cache[weights[0]] * base
            continue
        key = min(m, opposite[m])
        if ("pair", key) not in cache:
            along = None
            for d in range(3):
                step = lattice[key][d]
                if step:
                    term = velocity[d]
                    if along is None:
                        along = term if step == 1 else -term
                    else:
                        along = along + term if step == 1 else along - term
            cache[("pair", key)] = (base + 4.5 * along * along, 3.0 * along)
        even, odd = cache[("pair", key)]
        result[m] = cache[weights[m]] * (even + odd if m == key else even - odd)
    return result


def collide(f, solid):
    density, flows = moments(f)
    inverse = 1.0 / density
    velocity = [flow * inverse for flow in flows]
    feq = balance(relax_rate * density, velocity, range(19))
    post = [
        jnp.where(solid, f[opposite[m]], (1.0 - relax_rate) * f[m] + feq[m]) for m in range(19)
    ]
    return post, velocity


def kernel(sizes, *refs):
    nz, ny, nx = sizes
    (pop_hbm, solid_hbm, ports_hbm, conc_hbm, load_hbm, out, new_conc, new_load,
     pops, solid, ports, conc, load, post0, post1, speed, ypack, xpack,
     zrecv, yrecv, xrecv, zyrecv, zxrecv, yxrecv, corner, near, wrapped,
     sent_v, all_v, vel, load_sem, send_sem, recv_sem, near_sem, vsend, vrecv) = refs
    D, H, W = solid.shape
    ncy, ncx = conc.shape[2:]
    gz, gy, gx = lax.axis_index("gz"), lax.axis_index("gy"), lax.axis_index("gx")
    is_first, is_last = gz == 0, gz == nz - 1
    has_up, has_down = gz < nz - 1, gz > 0

    small = [
        pltpu.make_async_copy(a, b, load_sem.at[D + i])
        for i, (a, b) in enumerate(
            ((solid_hbm, solid), (ports_hbm, ports), (conc_hbm, conc), (load_hbm, load)))
    ]
    small[0].start()

    def plane_in(z):
        return pltpu.make_async_copy(pop_hbm.at[:, z], pops.at[:, z], load_sem.at[z])

    for z in range(D):
        plane_in(z).start()
    for copy in small[1:]:
        copy.start()

    def at(offset):
        dz, dy, dx = offset
        return {"gz": gz + dz, "gy": lax.rem(gy + dy + ny, ny), "gx": lax.rem(gx + dx + nx, nx)}

    flat = [(0, dy, dx) for dy in range(ny) for dx in range(nx) if dy or dx]
    cross = sorted({(dy % ny, dx % nx) for dy, dx in ((0, 0), (1, 0), (-1, 0), (0, 1), (0, -1))})
    barrier = pltpu.get_barrier_semaphore()

    def greet(offsets):
        for offset in offsets:
            pl.semaphore_signal(barrier, inc=1, device_id=at(offset), device_id_type=MESH)

    greet(flat)

    @pl.when(has_up)
    def _():
        greet([(1, dy, dx) for dy, dx in cross])

    @pl.when(has_down)
    def _():
        greet([(-1, dy, dx) for dy, dx in cross])

    lane = lax.broadcasted_iota(jnp.int32, (H, W), 1)
    row = lax.broadcasted_iota(jnp.int32, (H, W), 0)
    edge_lane = [lane == 0, lane == W - 1]
    edge_row = [row == 0, row == H - 1]
    first_mask = jnp.full((H, W), gz, jnp.int32) == 0
    last_mask = jnp.full((H, W), gz, jnp.int32) == nz - 1

    def rolled(x, step, axis):
        size = x.shape[axis]
        return pltpu.roll(x, step % size, axis)

    def blank(s):
        for it in range(ITERS):
            zrecv[it, s] = jnp.zeros(zrecv.shape[2:], jnp.float32)
            for at_member in range(4):
                if side(lattice[ZY[at_member]][0]) == s:
                    zyrecv[it, at_member] = jnp.zeros((H, W), jnp.float32)
                if side(lattice[ZX[at_member]][0]) == s:
                    zxrecv[it, at_member] = jnp.zeros((H, W), jnp.float32)

    for i in range(4):
        if i != 0:
            small[i].wait()

    @pl.when(is_first)
    def _():
        blank(0)
        for s in range(2):
            near[0, s] = jnp.full(near.shape[2:], feed_level[s], jnp.float32)

    @pl.when(is_last)
    def _():
        blank(1)
        near[1] = conc[...]

    posts = (post0, post1)

    def store_post(it, z, post, packs):
        where = posts[it]
        for m in range(19):
            where[SLOT[m], z] = post[m]
        for s in range(2):
            for i, m in enumerate(GROUPS[1][s]):
                edge = post[m][H - 1 :, :] if s == 0 else post[m][:1, :]
                ypack[it, s, i, pl.ds(z, 1), :] = edge
        new = []
        for s in range(2):
            acc = packs[s]
            for i, m in enumerate(GROUPS[2][s]):
                k = i * D + z
                acc = jnp.where(lane == k, pltpu.roll(post[m], k + 1 - s, 1), acc)
            new.append(acc)
        return tuple(new)

    def finish(it, packs):
        for s in range(2):
            xpack[it, s] = packs[s]

    def exchange(it):
        where = posts[it]
        moves = []
        for m in ZX:
            z = D - 1 if lattice[m][0] == 1 else 0
            moves.append((where.at[SLOT[m], z], zxrecv.at[it, m - ZX[0]], lattice[m]))
        for s in range(2):
            moves.append((xpack.at[it, s], xrecv.at[it, s], (0, 0, 1 - 2 * s)))
        for m in YX:
            s = side(lattice[m][1])
            moves.append((ypack.at[it, s, GROUPS[1][s].index(m)], yxrecv.at[it, m - YX[0]], lattice[m]))
        for m in ZY:
            z = D - 1 if lattice[m][0] == 1 else 0
            moves.append((where.at[SLOT[m], z], zyrecv.at[it, m - ZY[0]], lattice[m]))
        for s in range(2):
            z = D - 1 if s == 0 else 0
            moves.append((where.at[pl.ds(5 * s, 5), z], zrecv.at[it, s], (1 - 2 * s, 0, 0)))
        for s in range(2):
            moves.append((ypack.at[it, s], yrecv.at[it, s], (0, 1 - 2 * s, 0)))
        copies = {-1: [], 0: [], 1: []}
        for i, (src, dst, offset) in enumerate(moves):
            copies[offset[0]].append(
                pltpu.make_async_remote_copy(
                    src_ref=src, dst_ref=dst, send_sem=send_sem.at[it, i],
                    recv_sem=recv_sem.at[it, i], device_id=at(offset), device_id_type=MESH))
        return copies

    def run(copies, method, incoming=False):
        conds = {1: has_down, -1: has_up} if incoming else {1: has_up, -1: has_down}
        for dz in (1, -1):
            @pl.when(conds[dz])
            def _():
                for copy in copies[dz]:
                    getattr(copy, method)()
        for copy in copies[0]:
            getattr(copy, method)()

    small[0].wait()
    zero = jnp.zeros((H, W), jnp.float32)

    def first_plane(z, packs):
        plane_in(z).wait()
        f = [pops[m, z] for m in range(19)]
        post, velocity = collide(f, solid[z] == 1)
        if isinstance(z, int):
            for d in range(3):
                speed[0, d] = velocity[d]
        return store_post(0, z, post, packs)

    packs = lax.fori_loop(0, D - 1, first_plane, (zero, zero))
    packs = first_plane(D - 1, packs)
    finish(0, packs)

    up_down = jnp.where(has_up, len(cross), 0) + jnp.where(has_down, len(cross), 0)
    pl.semaphore_wait(barrier, len(flat) + up_down)

    moves0 = exchange(0)
    run(moves0, "start")
    ends = {1: [], -1: [], 0: []}
    for s in range(2):
        dz = 1 - 2 * s
        ends[dz].append(
            pltpu.make_async_remote_copy(
                src_ref=conc, dst_ref=near.at[s], send_sem=near_sem.at[0, s],
                recv_sem=near_sem.at[1, s], device_id=at((dz, 0, 0)), device_id_type=MESH))
    run(ends, "start")

    def arrive(it, copies):
        run(copies, "wait_recv", incoming=True)
        for m in YX:
            _, cy, cx = lattice[m]
            s = side(cy)
            own = rolled(yrecv[it, s, GROUPS[1][s].index(m)], cx, 1)
            far = rolled(yxrecv[it, m - YX[0]], cx, 1)
            corner[it, m - YX[0]] = jnp.where(edge_lane[side(cx)], far, own)

    def stream(it, z, place):
        where = posts[it]
        f = []
        for m in range(19):
            cz, cy, cx = lattice[m]
            beyond = (cz == 1 and place == "low") or (cz == -1 and place == "high")
            if beyond:
                s = side(cz)
                v = zrecv[it, s, GROUPS[0][s].index(m)]
            else:
                v = where[SLOT[m], z - cz]
            if cx:
                s = side(cx)
                if beyond:
                    column = rolled(zxrecv[it, m - ZX[0]], cx, 1)
                else:
                    k = GROUPS[2][s].index(m) * D + z - cz
                    column = pltpu.roll(xrecv[it, s], W - k if s == 0 else W - 1 - k, 1) \
                        if not (isinstance(k, int) and k == 0 and s == 0) else xrecv[it, s]
                v = jnp.where(edge_lane[s], column, rolled(v, cx, 1))
            if cy:
                s = side(cy)
                if beyond:
                    r = H - 1 if s == 0 else 0
                    line = zyrecv[it, m - ZY[0], r : r + 1, :]
                elif cx:
                    line = corner[it, m - YX[0], pl.ds(z, 1), :]
                else:
                    line = yrecv[it, s, GROUPS[1][s].index(m), pl.ds(z - cz, 1), :]
                v = jnp.where(edge_row[s], jnp.broadcast_to(line, (H, W)), rolled(v, cy, 0))
            f.append(v)
        if place == "low":
            inflow = equilibrium_at_inlet()
            opened = ports[0] == 1
            for m in GROUPS[0][0]:
                back = where[SLOT[opposite[m]], 0]
                f[m] = jnp.where(first_mask, jnp.where(opened, inflow[m], back), f[m])
        if place == "high":
            velocity = [speed[it, d] for d in range(3)]
            outflow = balance(base_density, velocity, GROUPS[0][1])
            opened = ports[1] == 1
            for m in GROUPS[0][1]:
                back = where[SLOT[opposite[m]], D - 1]
                f[m] = jnp.where(last_mask, jnp.where(opened, outflow[m], back), f[m])
        return f

    def planes(step, carry):
        carry = step(0, "low", carry)
        carry = lax.fori_loop(1, D - 1, lambda z, c: step(z, "mid", c), carry)
        return step(D - 1, "high", carry)

    arrive(0, moves0)

    def second_plane(z, place, packs):
        f = stream(0, z, place)
        post, velocity = collide(f, solid[z] == 1)
        if place == "high":
            for d in range(3):
                speed[1, d] = velocity[d]
        return store_post(1, z, post, packs)

    finish(1, planes(second_plane, (zero, zero)))
    moves1 = exchange(1)
    run(moves1, "start")

    run(ends, "wait_recv", incoming=True)
    source = lax.broadcasted_iota(jnp.int32, (ncx, ncx), 0)
    target = lax.broadcasted_iota(jnp.int32, (ncx, ncx), 1)
    ahead = jnp.where(target == ncx - 1, 0, target + 1)
    behind = jnp.where(target == 0, ncx - 1, target - 1)
    take_after = (source == ahead).astype(jnp.float32)
    take_before = (source == behind).astype(jnp.float32)

    def exact_dot(a, b):
        return jnp.dot(a, b, precision=lax.Precision.HIGHEST, preferred_element_type=jnp.float32)

    diffs = []
    for s in range(2):
        c = conc[s, 0]
        wrapped[s, 1 : ncy + 1, :] = c
        wrapped[s, 0:1, :] = conc[s, 0, ncy - 1 : ncy, :]
        wrapped[s, ncy + 1 : ncy + 2, :] = conc[s, 0, 0:1, :]
        pairs = [
            (near[0, s, 0], near[1, s, 0]),
            (wrapped[s, 0:ncy, :], wrapped[s, 2 : ncy + 2, :]),
            (exact_dot(c, take_before), exact_dot(c, take_after)),
        ]
        curvature = sum(b + a - 2.0 * c for b, a in pairs)
        rate = uptake_rate[s] * (affinity[s] * c - load[s, 0])
        new_load[s, 0] = load[s, 0] + rate
        diffs.append((c - phase_ratio * rate + spread_base[s] * curvature, curvature,
                      [(c - b, a - c) for b, a in pairs]))

    arrive(1, moves1)

    def last_plane(z, place, totals):
        f = stream(1, z, place)
        for m in range(19):
            out[m, z] = f[m]
        pore = solid[z] == 0
        return tuple(t + jnp.where(pore, flow, 0.0) for t, flow in zip(totals, momentum(f)))

    totals = planes(last_plane, (zero, zero, zero))
    sums = zero
    for d in range(3):
        line = jnp.sum(totals[d], axis=0, keepdims=True)
        sums = jnp.where(row == d, jnp.broadcast_to(line, (H, W)), sums)
    wide = sent_v.shape[1]
    voxel = lax.broadcasted_iota(jnp.int32, (W, wide), 0)
    cell = lax.broadcasted_iota(jnp.int32, (W, wide), 1) - gx * (W // CELL)
    pick = ((voxel >= cell * CELL) & (voxel < cell * CELL + CELL)).astype(jnp.float32)
    sent_v[...] = exact_dot(sums, pick) * (1.0 / (CELL * CELL * CELL * base_density))
    tell = [
        pltpu.make_async_remote_copy(
            src_ref=sent_v, dst_ref=all_v.at[gy, gx], send_sem=vsend.at[i],
            recv_sem=vrecv.at[i], device_id=at(offset), device_id_type=MESH)
        for i, offset in enumerate(flat)
    ]
    for copy in tell:
        copy.start()
    all_v[gy, gx] = sent_v[...]
    run(moves0, "wait_send")
    run(moves1, "wait_send")
    run(ends, "wait_send")
    for copy in tell:
        copy.wait_recv()

    for y in range(ny):
        total = all_v[y, 0]
        for x in range(1, nx):
            total = total + all_v[y, x]
        for d in range(3):
            vel[d, y : y + 1, :] = total[d : d + 1, :]
    courant = [CELL * vel[d][:, :ncx] for d in range(3)]
    reach = jnp.abs(courant[0]) + jnp.abs(courant[1]) + jnp.abs(courant[2])
    for s in range(2):
        value, curvature, steps = diffs[s]
        for d in range(3):
            low, high = steps[d]
            value = value - jnp.maximum(courant[d], 0.0) * low - jnp.minimum(courant[d], 0.0) * high
        new_conc[s, 0] = value + spread_length * reach * curvature
    for copy in tell:
        copy.wait_send()


def hand_out(*refs):
    copies = [pltpu.make_async_copy(refs[i], refs[3 + i], refs[6].at[i]) for i in range(3)]
    for copy in copies:
        copy.start()
    for copy in copies:
        copy.wait()


def equilibrium_at_inlet():
    result = {}
    for m in GROUPS[0][0]:
        along = inlet_speed
        result[m] = weights[m] * base_density * (
            1.0 + 3.0 * along + 4.5 * along * along - 1.5 * inlet_speed * inlet_speed)
    return result


def solution(mesh):
    sizes = tuple(mesh.shape[a] for a in ("gz", "gy", "gx"))
    nz, ny, nx = sizes

    def body(populations, solid, ports, concentration, loaded):
        D, H, W = solid.shape
        ncy, ncx = concentration.shape[2:]
        assert D == CELL and H == CELL and W % 128 == 0 and 5 * D <= W
        wide = -(-ncx // 128) * 128
        f32 = jnp.float32
        tile = (H, W)
        anywhere = pl.BlockSpec(memory_space=pl.ANY)
        inside = pl.BlockSpec(memory_space=pltpu.VMEM)
        results = (populations, concentration, loaded)
        made = pl.pallas_call(
            functools.partial(kernel, sizes),
            out_shape=tuple(pltpu.VMEM(a.shape, f32) for a in results),
            in_specs=[anywhere] * 5,
            out_specs=(inside,) * 3,
            scratch_shapes=[
                pltpu.VMEM(populations.shape, f32),
                pltpu.VMEM(solid.shape, jnp.int32),
                pltpu.VMEM(ports.shape, jnp.int32),
                pltpu.VMEM(concentration.shape, f32),
                pltpu.VMEM(loaded.shape, f32),
                pltpu.VMEM((19, D) + tile, f32),
                pltpu.VMEM((19, D) + tile, f32),
                pltpu.VMEM((ITERS, 3) + tile, f32),
                pltpu.VMEM((ITERS, 2, 5, D, W), f32),
                pltpu.VMEM((ITERS, 2) + tile, f32),
                pltpu.VMEM((ITERS, 2, 5) + tile, f32),
                pltpu.VMEM((ITERS, 2, 5, D, W), f32),
                pltpu.VMEM((ITERS, 2) + tile, f32),
                pltpu.VMEM((ITERS, 4) + tile, f32),
                pltpu.VMEM((ITERS, 4) + tile, f32),
                pltpu.VMEM((ITERS, 4, D, W), f32),
                pltpu.VMEM((ITERS, 4, D, W), f32),
                pltpu.VMEM((2,) + concentration.shape, f32),
                pltpu.VMEM((2, ncy + 2, ncx), f32),
                pltpu.VMEM((8, wide), f32),
                pltpu.VMEM((ny, nx, 8, wide), f32),
                pltpu.VMEM((3, ncy, wide), f32),
                pltpu.SemaphoreType.DMA((D + 4,)),
                pltpu.SemaphoreType.DMA((ITERS, 18)),
                pltpu.SemaphoreType.DMA((ITERS, 18)),
                pltpu.SemaphoreType.DMA((2, 2)),
                pltpu.SemaphoreType.DMA((ny * nx - 1,)),
                pltpu.SemaphoreType.DMA((ny * nx - 1,)),
            ],
            compiler_params=pltpu.CompilerParams(collective_id=0, has_side_effects=True),
        )(populations, solid, ports, concentration, loaded)
        return pl.pallas_call(
            hand_out,
            out_shape=tuple(jax.ShapeDtypeStruct(a.shape, f32) for a in results),
            in_specs=[inside] * 3,
            out_specs=(anywhere,) * 3,
            scratch_shapes=[pltpu.SemaphoreType.DMA((3,))],
        )(*[pltpu.with_memory_space_constraint(a, pltpu.VMEM) for a in made])

    placed = (
        P(None, "gz", "gy", "gx"),
        P("gz", "gy", "gx"),
        P(None, "gy", "gx"),
        P(None, "gz", None, None),
        P(None, "gz", None, None),
    )
    return jax.shard_map(
        body,
        mesh=mesh,
        in_specs=placed,
        out_specs=(P(None, "gz", "gy", "gx"), P(None, "gz", None, None), P(None, "gz", None, None)),
        check_vma=False,
    )
```

```python
import functools

import jax
import jax.numpy as jnp
from jax import lax
from jax.experimental import pallas as pl
from jax.experimental.pallas import tpu as pltpu
from jax.sharding import PartitionSpec as P

ITERS = 2
CELL = 8
MESH = pl.DeviceIdType.MESH

lattice = [
    (0, 0, 0),
    (1, 0, 0),
    (-1, 0, 0),
    (0, 1, 0),
    (0, -1, 0),
    (0, 0, 1),
    (0, 0, -1),
    (1, 1, 0),
    (-1, -1, 0),
    (1, -1, 0),
    (-1, 1, 0),
    (1, 0, 1),
    (-1, 0, -1),
    (1, 0, -1),
    (-1, 0, 1),
    (0, 1, 1),
    (0, -1, -1),
    (0, 1, -1),
    (0, -1, 1),
]
opposite = [0, 2, 1, 4, 3, 6, 5, 8, 7, 10, 9, 12, 11, 14, 13, 16, 15, 18, 17]
weights = [1.0 / 3.0] + [1.0 / 18.0] * 6 + [1.0 / 36.0] * 12
relax_rate = 1.25
base_density = 36.0
inlet_speed = 0.05
spread_base = (0.03, 0.06)
spread_length = 0.1
uptake_rate = (0.3, 0.6)
affinity = (2.0, 0.5)
phase_ratio = 0.5
feed_level = (1.0, 0.5)

GROUPS = [[[m for m in range(19) if lattice[m][d] == s] for s in (1, -1)] for d in range(3)]
ORDER = GROUPS[0][0] + GROUPS[0][1] + [m for m in range(19) if lattice[m][0] == 0]
SLOT = {m: i for i, m in enumerate(ORDER)}
ZY, ZX, YX = (7, 8, 9, 10), (11, 12, 13, 14), (15, 16, 17, 18)


def side(step):
    return 0 if step == 1 else 1


def moments(f):
    density = f[0]
    for member in range(1, 19):
        density = density + f[member]
    return density, momentum(f)


def momentum(f):
    flows = []
    for d in range(3):
        total = None
        for a, b in zip(GROUPS[d][0], [opposite[m] for m in GROUPS[d][0]]):
            part = f[a] - f[b]
            total = part if total is None else total + part
        flows.append(total)
    return flows


def balance(scale, velocity, members):
    square = velocity[0] * velocity[0] + velocity[1] * velocity[1] + velocity[2] * velocity[2]
    base = 1.0 - 1.5 * square
    cache, result = {}, {}
    for w in set(weights[m] for m in members):
        cache[w] = scale * w
    for m in members:
        if m == 0:
            result[m] = cache[weights[0]] * base
            continue
        key = min(m, opposite[m])
        if ("pair", key) not in cache:
            along = None
            for d in range(3):
                step = lattice[key][d]
                if step:
                    term = velocity[d]
                    if along is None:
                        along = term if step == 1 else -term
                    else:
                        along = along + term if step == 1 else along - term
            cache[("pair", key)] = (base + 4.5 * along * along, 3.0 * along)
        even, odd = cache[("pair", key)]
        result[m] = cache[weights[m]] * (even + odd if m == key else even - odd)
    return result


def collide(f, solid):
    density, flows = moments(f)
    inverse = 1.0 / density
    velocity = [flow * inverse for flow in flows]
    feq = balance(relax_rate * density, velocity, range(19))
    post = [
        jnp.where(solid, f[opposite[m]], (1.0 - relax_rate) * f[m] + feq[m]) for m in range(19)
    ]
    return post, velocity


def kernel(sizes, *refs):
    nz, ny, nx = sizes
    (pop_hbm, solid_hbm, ports_hbm, conc_hbm, load_hbm, out, new_conc, new_load,
     pops, solid, ports, conc, load, post0, post1, speed, ypack, xpack,
     zyline, zrecv, yrecv, xrecv, zyrecv, zxrecv, yxrecv, corner, near, wrapped,
     sent_v, all_v, vel, load_sem, send_sem, recv_sem, near_sem, vsend, vrecv) = refs
    D, H, W = solid.shape
    ncy, ncx = conc.shape[2:]
    gz, gy, gx = lax.axis_index("gz"), lax.axis_index("gy"), lax.axis_index("gx")
    is_first, is_last = gz == 0, gz == nz - 1
    has_up, has_down = gz < nz - 1, gz > 0

    small = [
        pltpu.make_async_copy(a, b, load_sem.at[D + i])
        for i, (a, b) in enumerate(
            ((solid_hbm, solid), (ports_hbm, ports), (conc_hbm, conc), (load_hbm, load)))
    ]
    small[0].start()

    def plane_in(z):
        return pltpu.make_async_copy(pop_hbm.at[:, z], pops.at[:, z], load_sem.at[z])

    for z in range(D):
        plane_in(z).start()
    for copy in small[1:]:
        copy.start()

    def at(offset):
        dz, dy, dx = offset
        return {"gz": gz + dz, "gy": lax.rem(gy + dy + ny, ny), "gx": lax.rem(gx + dx + nx, nx)}

    flat = [(0, dy, dx) for dy in range(ny) for dx in range(nx) if dy or dx]
    cross = sorted({(dy % ny, dx % nx) for dy, dx in ((0, 0), (1, 0), (-1, 0), (0, 1), (0, -1))})
    barrier = pltpu.get_barrier_semaphore()

    def greet(offsets):
        for offset in offsets:
            pl.semaphore_signal(barrier, inc=1, device_id=at(offset), device_id_type=MESH)

    greet(flat)

    @pl.when(has_up)
    def _():
        greet([(1, dy, dx) for dy, dx in cross])

    @pl.when(has_down)
    def _():
        greet([(-1, dy, dx) for dy, dx in cross])

    lane = lax.broadcasted_iota(jnp.int32, (H, W), 1)
    row = lax.broadcasted_iota(jnp.int32, (H, W), 0)
    edge_lane = [lane == 0, lane == W - 1]
    edge_row = [row == 0, row == H - 1]
    first_mask = jnp.full((H, W), gz, jnp.int32) == 0
    last_mask = jnp.full((H, W), gz, jnp.int32) == nz - 1

    def rolled(x, step, axis):
        size = x.shape[axis]
        return pltpu.roll(x, step % size, axis)

    def blank(s):
        for it in range(ITERS):
            zrecv[it, s] = jnp.zeros(zrecv.shape[2:], jnp.float32)
            for at_member in range(4):
                if side(lattice[ZY[at_member]][0]) == s:
                    zyrecv[it, at_member] = jnp.zeros((1, W), jnp.float32)
                if side(lattice[ZX[at_member]][0]) == s:
                    zxrecv[it, at_member] = jnp.zeros((H, W), jnp.float32)

    for i in range(4):
        if i != 0:
            small[i].wait()

    @pl.when(is_first)
    def _():
        blank(0)
        for s in range(2):
            near[0, s] = jnp.full(near.shape[2:], feed_level[s], jnp.float32)

    @pl.when(is_last)
    def _():
        blank(1)
        near[1] = conc[...]

    posts = (post0, post1)

    def store_post(it, z, post, packs):
        where = posts[it]
        for m in range(19):
            where[SLOT[m], z] = post[m]
        for s in range(2):
            for i, m in enumerate(GROUPS[1][s]):
                edge = post[m][H - 1 :, :] if s == 0 else post[m][:1, :]
                ypack[it, s, i, pl.ds(z, 1), :] = edge
        if isinstance(z, int):
            for m in ZY:
                cz, cy, _ = lattice[m]
                if z == (D - 1 if cz == 1 else 0):
                    zyline[it, m - ZY[0]] = post[m][H - 1 :, :] if cy == 1 else post[m][:1, :]
        new = []
        for s in range(2):
            acc = packs[s]
            for i, m in enumerate(GROUPS[2][s]):
                k = i * D + z
                acc = jnp.where(lane == k, pltpu.roll(post[m], k + 1 - s, 1), acc)
            new.append(acc)
        return tuple(new)

    def finish(it, packs):
        for s in range(2):
            xpack[it, s] = packs[s]

    def exchange(it):
        where = posts[it]
        moves = []
        for s in range(2):
            moves.append((xpack.at[it, s], xrecv.at[it, s], (0, 0, 1 - 2 * s)))
        for m in ZX:
            z = D - 1 if lattice[m][0] == 1 else 0
            moves.append((where.at[SLOT[m], z], zxrecv.at[it, m - ZX[0]], lattice[m]))
        for m in YX:
            s = side(lattice[m][1])
            moves.append((ypack.at[it, s, GROUPS[1][s].index(m)], yxrecv.at[it, m - YX[0]], lattice[m]))
        for m in ZY:
            moves.append((zyline.at[it, m - ZY[0]], zyrecv.at[it, m - ZY[0]], lattice[m]))
        for s in range(2):
            z = D - 1 if s == 0 else 0
            moves.append((where.at[pl.ds(5 * s, 5), z], zrecv.at[it, s], (1 - 2 * s, 0, 0)))
        for s in range(2):
            moves.append((ypack.at[it, s], yrecv.at[it, s], (0, 1 - 2 * s, 0)))
        copies = {-1: [], 0: [], 1: []}
        for i, (src, dst, offset) in enumerate(moves):
            copies[offset[0]].append(
                pltpu.make_async_remote_copy(
                    src_ref=src, dst_ref=dst, send_sem=send_sem.at[it, i],
                    recv_sem=recv_sem.at[it, i], device_id=at(offset), device_id_type=MESH))
        return copies

    def run(copies, method, incoming=False):
        conds = {1: has_down, -1: has_up} if incoming else {1: has_up, -1: has_down}
        for copy in copies.get(0, ()):
            getattr(copy, method)()
        for dz in (1, -1):
            if copies.get(dz):
                @pl.when(conds[dz])
                def _():
                    for copy in copies[dz]:
                        getattr(copy, method)()

    def cross_arrive(copies):
        run({1: copies[1], -1: copies[-1]}, "wait_recv", incoming=True)

    small[0].wait()
    zero = jnp.zeros((H, W), jnp.float32)

    def first_plane(z, packs):
        plane_in(z).wait()
        f = [pops[m, z] for m in range(19)]
        post, velocity = collide(f, solid[z] == 1)
        if isinstance(z, int) and z == D - 1:
            for d in range(3):
                speed[0, d] = velocity[d]
        return store_post(0, z, post, packs)

    packs = first_plane(0, (zero, zero))
    packs = lax.fori_loop(1, D - 1, first_plane, packs)
    packs = first_plane(D - 1, packs)
    finish(0, packs)

    up_down = jnp.where(has_up, len(cross), 0) + jnp.where(has_down, len(cross), 0)
    pl.semaphore_wait(barrier, len(flat) + up_down)

    moves0 = exchange(0)
    run(moves0, "start")
    ends = {1: [], -1: [], 0: []}
    for s in range(2):
        dz = 1 - 2 * s
        ends[dz].append(
            pltpu.make_async_remote_copy(
                src_ref=conc, dst_ref=near.at[s], send_sem=near_sem.at[0, s],
                recv_sem=near_sem.at[1, s], device_id=at((dz, 0, 0)), device_id_type=MESH))
    run(ends, "start")

    def arrive(it, copies):
        run({0: copies[0]}, "wait_recv")
        for m in YX:
            _, cy, cx = lattice[m]
            s = side(cy)
            own = rolled(yrecv[it, s, GROUPS[1][s].index(m)], cx, 1)
            far = rolled(yxrecv[it, m - YX[0]], cx, 1)
            corner[it, m - YX[0]] = jnp.where(edge_lane[side(cx)], far, own)

    def stream(it, z, place):
        where = posts[it]
        f = []
        for m in range(19):
            cz, cy, cx = lattice[m]
            beyond = (cz == 1 and place == "low") or (cz == -1 and place == "high")
            if beyond:
                s = side(cz)
                v = zrecv[it, s, GROUPS[0][s].index(m)]
            else:
                v = where[SLOT[m], z - cz]
            if cx:
                s = side(cx)
                if beyond:
                    column = rolled(zxrecv[it, m - ZX[0]], cx, 1)
                else:
                    k = GROUPS[2][s].index(m) * D + z - cz
                    column = pltpu.roll(xrecv[it, s], W - k if s == 0 else W - 1 - k, 1) \
                        if not (isinstance(k, int) and k == 0 and s == 0) else xrecv[it, s]
                v = jnp.where(edge_lane[s], column, rolled(v, cx, 1))
            if cy:
                s = side(cy)
                if beyond:
                    line = zyrecv[it, m - ZY[0]]
                elif cx:
                    line = corner[it, m - YX[0], pl.ds(z, 1), :]
                else:
                    line = yrecv[it, s, GROUPS[1][s].index(m), pl.ds(z - cz, 1), :]
                v = jnp.where(edge_row[s], jnp.broadcast_to(line, (H, W)), rolled(v, cy, 0))
            f.append(v)
        if place == "low":
            inflow = equilibrium_at_inlet()
            opened = ports[0] == 1
            for m in GROUPS[0][0]:
                back = where[SLOT[opposite[m]], 0]
                f[m] = jnp.where(first_mask, jnp.where(opened, inflow[m], back), f[m])
        if place == "high":
            velocity = [speed[it, d] for d in range(3)]
            outflow = balance(base_density, velocity, GROUPS[0][1])
            opened = ports[1] == 1
            for m in GROUPS[0][1]:
                back = where[SLOT[opposite[m]], D - 1]
                f[m] = jnp.where(last_mask, jnp.where(opened, outflow[m], back), f[m])
        return f

    def planes(step, carry, crossing):
        carry = lax.fori_loop(1, D - 1, lambda z, c: step(z, "mid", c), carry)
        crossing()
        carry = step(0, "low", carry)
        return step(D - 1, "high", carry)

    arrive(0, moves0)

    def second_plane(z, place, packs):
        f = stream(0, z, place)
        post, velocity = collide(f, solid[z] == 1)
        if place == "high":
            for d in range(3):
                speed[1, d] = velocity[d]
        return store_post(1, z, post, packs)

    finish(1, planes(second_plane, (zero, zero), lambda: cross_arrive(moves0)))
    moves1 = exchange(1)
    run(moves1, "start")

    run(ends, "wait_recv", incoming=True)
    source = lax.broadcasted_iota(jnp.int32, (ncx, ncx), 0)
    target = lax.broadcasted_iota(jnp.int32, (ncx, ncx), 1)
    ahead = jnp.where(target == ncx - 1, 0, target + 1)
    behind = jnp.where(target == 0, ncx - 1, target - 1)
    take_after = (source == ahead).astype(jnp.float32)
    take_before = (source == behind).astype(jnp.float32)

    def exact_dot(a, b):
        return jnp.dot(a, b, precision=lax.Precision.HIGHEST, preferred_element_type=jnp.float32)

    diffs = []
    for s in range(2):
        c = conc[s, 0]
        wrapped[s, 1 : ncy + 1, :] = c
        wrapped[s, 0:1, :] = conc[s, 0, ncy - 1 : ncy, :]
        wrapped[s, ncy + 1 : ncy + 2, :] = conc[s, 0, 0:1, :]
        pairs = [
            (near[0, s, 0], near[1, s, 0]),
            (wrapped[s, 0:ncy, :], wrapped[s, 2 : ncy + 2, :]),
            (exact_dot(c, take_before), exact_dot(c, take_after)),
        ]
        curvature = sum(b + a - 2.0 * c for b, a in pairs)
        rate = uptake_rate[s] * (affinity[s] * c - load[s, 0])
        new_load[s, 0] = load[s, 0] + rate
        diffs.append((c - phase_ratio * rate + spread_base[s] * curvature, curvature,
                      [(c - b, a - c) for b, a in pairs]))

    arrive(1, moves1)

    def last_plane(z, place, totals):
        f = stream(1, z, place)
        for m in range(19):
            out[m, z] = f[m]
        pore = solid[z] == 0
        return tuple(t + jnp.where(pore, flow, 0.0) for t, flow in zip(totals, momentum(f)))

    totals = planes(last_plane, (zero, zero, zero), lambda: cross_arrive(moves1))
    sums = zero
    for d in range(3):
        line = jnp.sum(totals[d], axis=0, keepdims=True)
        sums = jnp.where(row == d, jnp.broadcast_to(line, (H, W)), sums)
    wide = sent_v.shape[2]
    voxel = lax.broadcasted_iota(jnp.int32, (W, wide), 0)
    cell = lax.broadcasted_iota(jnp.int32, (W, wide), 1) - gx * (W // CELL)
    pick = ((voxel >= cell * CELL) & (voxel < cell * CELL + CELL)).astype(jnp.float32)
    mine = exact_dot(sums, pick) * (1.0 / (CELL * CELL * CELL * base_density))
    for d in range(3):
        sent_v[d] = mine[d : d + 1, :]
    tell = [
        pltpu.make_async_remote_copy(
            src_ref=sent_v, dst_ref=all_v.at[gy, gx], send_sem=vsend.at[i],
            recv_sem=vrecv.at[i], device_id=at(offset), device_id_type=MESH)
        for i, offset in enumerate(flat)
    ]
    for copy in tell:
        copy.start()
    all_v[gy, gx] = sent_v[...]
    run(moves0, "wait_send")
    run(moves1, "wait_send")
    run(ends, "wait_send")
    for copy in tell:
        copy.wait_recv()

    for y in range(ny):
        total = all_v[y, 0]
        for x in range(1, nx):
            total = total + all_v[y, x]
        for d in range(3):
            vel[d, y : y + 1, :] = total[d]
    courant = [CELL * vel[d][:, :ncx] for d in range(3)]
    reach = jnp.abs(courant[0]) + jnp.abs(courant[1]) + jnp.abs(courant[2])
    for s in range(2):
        value, curvature, steps = diffs[s]
        for d in range(3):
            low, high = steps[d]
            value = value - jnp.maximum(courant[d], 0.0) * low - jnp.minimum(courant[d], 0.0) * high
        new_conc[s, 0] = value + spread_length * reach * curvature
    for copy in tell:
        copy.wait_send()


def hand_out(*refs):
    copies = [pltpu.make_async_copy(refs[i], refs[3 + i], refs[6].at[i]) for i in range(3)]
    for copy in copies:
        copy.start()
    for copy in copies:
        copy.wait()


def equilibrium_at_inlet():
    result = {}
    for m in GROUPS[0][0]:
        along = inlet_speed
        result[m] = weights[m] * base_density * (
            1.0 + 3.0 * along + 4.5 * along * along - 1.5 * inlet_speed * inlet_speed)
    return result


def solution(mesh):
    sizes = tuple(mesh.shape[a] for a in ("gz", "gy", "gx"))
    nz, ny, nx = sizes

    def body(populations, solid, ports, concentration, loaded):
        D, H, W = solid.shape
        ncy, ncx = concentration.shape[2:]
        assert D == CELL and H == CELL and W % 128 == 0 and 5 * D <= W
        wide = -(-ncx // 128) * 128
        f32 = jnp.float32
        tile = (H, W)
        anywhere = pl.BlockSpec(memory_space=pl.ANY)
        inside = pl.BlockSpec(memory_space=pltpu.VMEM)
        results = (populations, concentration, loaded)
        made = pl.pallas_call(
            functools.partial(kernel, sizes),
            out_shape=tuple(pltpu.VMEM(a.shape, f32) for a in results),
            in_specs=[anywhere] * 5,
            out_specs=(inside,) * 3,
            scratch_shapes=[
                pltpu.VMEM(populations.shape, f32),
                pltpu.VMEM(solid.shape, jnp.int32),
                pltpu.VMEM(ports.shape, jnp.int32),
                pltpu.VMEM(concentration.shape, f32),
                pltpu.VMEM(loaded.shape, f32),
                pltpu.VMEM((19, D) + tile, f32),
                pltpu.VMEM((19, D) + tile, f32),
                pltpu.VMEM((ITERS, 3) + tile, f32),
                pltpu.VMEM((ITERS, 2, 5, D, W), f32),
                pltpu.VMEM((ITERS, 2) + tile, f32),
                pltpu.VMEM((ITERS, 4, 1, W), f32),
                pltpu.VMEM((ITERS, 2, 5) + tile, f32),
                pltpu.VMEM((ITERS, 2, 5, D, W), f32),
                pltpu.VMEM((ITERS, 2) + tile, f32),
                pltpu.VMEM((ITERS, 4, 1, W), f32),
                pltpu.VMEM((ITERS, 4) + tile, f32),
                pltpu.VMEM((ITERS, 4, D, W), f32),
                pltpu.VMEM((ITERS, 4, D, W), f32),
                pltpu.VMEM((2,) + concentration.shape, f32),
                pltpu.VMEM((2, ncy + 2, ncx), f32),
                pltpu.VMEM((3, 1, wide), f32),
                pltpu.VMEM((ny, nx, 3, 1, wide), f32),
                pltpu.VMEM((3, ncy, wide), f32),
                pltpu.SemaphoreType.DMA((D + 4,)),
                pltpu.SemaphoreType.DMA((ITERS, 18)),
                pltpu.SemaphoreType.DMA((ITERS, 18)),
                pltpu.SemaphoreType.DMA((2, 2)),
                pltpu.SemaphoreType.DMA((ny * nx - 1,)),
                pltpu.SemaphoreType.DMA((ny * nx - 1,)),
            ],
            compiler_params=pltpu.CompilerParams(collective_id=0, has_side_effects=True),
        )(populations, solid, ports, concentration, loaded)
        return pl.pallas_call(
            hand_out,
            out_shape=tuple(jax.ShapeDtypeStruct(a.shape, f32) for a in results),
            in_specs=[inside] * 3,
            out_specs=(anywhere,) * 3,
            scratch_shapes=[pltpu.SemaphoreType.DMA((3,))],
        )(*[pltpu.with_memory_space_constraint(a, pltpu.VMEM) for a in made])

    placed = (
        P(None, "gz", "gy", "gx"),
        P("gz", "gy", "gx"),
        P(None, "gy", "gx"),
        P(None, "gz", None, None),
        P(None, "gz", None, None),
    )
    return jax.shard_map(
        body,
        mesh=mesh,
        in_specs=placed,
        out_specs=(P(None, "gz", "gy", "gx"), P(None, "gz", None, None), P(None, "gz", None, None)),
        check_vma=False,
    )
```

```python
import functools

import jax
import jax.numpy as jnp
from jax import lax
from jax.experimental import pallas as pl
from jax.experimental.pallas import tpu as pltpu
from jax.sharding import PartitionSpec as P

ITERS = 2
CELL = 8
MESH = pl.DeviceIdType.MESH

lattice = [
    (0, 0, 0),
    (1, 0, 0),
    (-1, 0, 0),
    (0, 1, 0),
    (0, -1, 0),
    (0, 0, 1),
    (0, 0, -1),
    (1, 1, 0),
    (-1, -1, 0),
    (1, -1, 0),
    (-1, 1, 0),
    (1, 0, 1),
    (-1, 0, -1),
    (1, 0, -1),
    (-1, 0, 1),
    (0, 1, 1),
    (0, -1, -1),
    (0, 1, -1),
    (0, -1, 1),
]
opposite = [0, 2, 1, 4, 3, 6, 5, 8, 7, 10, 9, 12, 11, 14, 13, 16, 15, 18, 17]
weights = [1.0 / 3.0] + [1.0 / 18.0] * 6 + [1.0 / 36.0] * 12
relax_rate = 1.25
base_density = 36.0
inlet_speed = 0.05
spread_base = (0.03, 0.06)
spread_length = 0.1
uptake_rate = (0.3, 0.6)
affinity = (2.0, 0.5)
phase_ratio = 0.5
feed_level = (1.0, 0.5)

GROUPS = [[[m for m in range(19) if lattice[m][d] == s] for s in (1, -1)] for d in range(3)]
ORDER = GROUPS[0][0] + GROUPS[0][1] + [m for m in range(19) if lattice[m][0] == 0]
SLOT = {m: i for i, m in enumerate(ORDER)}
ZY, ZX, YX = (7, 8, 9, 10), (11, 12, 13, 14), (15, 16, 17, 18)


def side(step):
    return 0 if step == 1 else 1


def moments(f):
    density = f[0]
    for member in range(1, 19):
        density = density + f[member]
    return density, momentum(f)


def momentum(f):
    flows = []
    for d in range(3):
        total = None
        for a, b in zip(GROUPS[d][0], [opposite[m] for m in GROUPS[d][0]]):
            part = f[a] - f[b]
            total = part if total is None else total + part
        flows.append(total)
    return flows


def balance(scale, velocity, members):
    square = velocity[0] * velocity[0] + velocity[1] * velocity[1] + velocity[2] * velocity[2]
    base = 1.0 - 1.5 * square
    cache, result = {}, {}
    for w in set(weights[m] for m in members):
        cache[w] = scale * w
    for m in members:
        if m == 0:
            result[m] = cache[weights[0]] * base
            continue
        key = min(m, opposite[m])
        if ("pair", key) not in cache:
            along = None
            for d in range(3):
                step = lattice[key][d]
                if step:
                    term = velocity[d]
                    if along is None:
                        along = term if step == 1 else -term
                    else:
                        along = along + term if step == 1 else along - term
            cache[("pair", key)] = (base + 4.5 * along * along, 3.0 * along)
        even, odd = cache[("pair", key)]
        result[m] = cache[weights[m]] * (even + odd if m == key else even - odd)
    return result


def collide(f, solid):
    density, flows = moments(f)
    inverse = 1.0 / density
    velocity = [flow * inverse for flow in flows]
    feq = balance(relax_rate * density, velocity, range(19))
    post = [
        jnp.where(solid, f[opposite[m]], (1.0 - relax_rate) * f[m] + feq[m]) for m in range(19)
    ]
    return post, velocity


def kernel(sizes, *refs):
    nz, ny, nx = sizes
    (pop_hbm, solid_hbm, ports_hbm, conc_hbm, load_hbm, out, new_conc, new_load,
     pops, solid, ports, conc, load, post0, post1, speed, ypack, xpack,
     zyline, zrecv, yrecv, xrecv, zyrecv, zxrecv, yxrecv, corner, near, wrapped,
     sent_v, all_v, vel, load_sem, send_sem, recv_sem, near_sem, vsend, vrecv) = refs
    D, H, W = solid.shape
    ncy, ncx = conc.shape[2:]
    gz, gy, gx = lax.axis_index("gz"), lax.axis_index("gy"), lax.axis_index("gx")
    is_first, is_last = gz == 0, gz == nz - 1
    has_up, has_down = gz < nz - 1, gz > 0

    small = [
        pltpu.make_async_copy(a, b, load_sem.at[D + i])
        for i, (a, b) in enumerate(
            ((solid_hbm, solid), (ports_hbm, ports), (conc_hbm, conc), (load_hbm, load)))
    ]
    small[0].start()

    def plane_in(z):
        return pltpu.make_async_copy(pop_hbm.at[:, z], pops.at[:, z], load_sem.at[z])

    for z in range(D):
        plane_in(z).start()
    for copy in small[1:]:
        copy.start()

    def at(offset):
        dz, dy, dx = offset
        return {"gz": gz + dz, "gy": lax.rem(gy + dy + ny, ny), "gx": lax.rem(gx + dx + nx, nx)}

    flat = [(0, dy, dx) for dy in range(ny) for dx in range(nx) if dy or dx]
    cross = sorted({(dy % ny, dx % nx) for dy, dx in ((0, 0), (1, 0), (-1, 0), (0, 1), (0, -1))})
    barrier = pltpu.get_barrier_semaphore()

    def greet(offsets):
        for offset in offsets:
            pl.semaphore_signal(barrier, inc=1, device_id=at(offset), device_id_type=MESH)

    greet(flat)

    @pl.when(has_up)
    def _():
        greet([(1, dy, dx) for dy, dx in cross])

    @pl.when(has_down)
    def _():
        greet([(-1, dy, dx) for dy, dx in cross])

    lane = lax.broadcasted_iota(jnp.int32, (H, W), 1)
    row = lax.broadcasted_iota(jnp.int32, (H, W), 0)
    edge_lane = [lane == 0, lane == W - 1]
    edge_row = [row == 0, row == H - 1]
    first_mask = jnp.full((H, W), gz, jnp.int32) == 0
    last_mask = jnp.full((H, W), gz, jnp.int32) == nz - 1

    def rolled(x, step, axis):
        size = x.shape[axis]
        return pltpu.roll(x, step % size, axis)

    def blank(s):
        for it in range(ITERS):
            zrecv[it, s] = jnp.zeros(zrecv.shape[2:], jnp.float32)
            for at_member in range(4):
                if side(lattice[ZY[at_member]][0]) == s:
                    zyrecv[it, at_member] = jnp.zeros((1, W), jnp.float32)
                if side(lattice[ZX[at_member]][0]) == s:
                    zxrecv[it, at_member] = jnp.zeros((H, W), jnp.float32)

    for i in range(4):
        if i != 0:
            small[i].wait()

    @pl.when(is_first)
    def _():
        blank(0)
        for s in range(2):
            near[0, s] = jnp.full(near.shape[2:], feed_level[s], jnp.float32)

    @pl.when(is_last)
    def _():
        blank(1)
        near[1] = conc[...]

    posts = (post0, post1)

    def store_post(it, z, post, packs):
        where = posts[it]
        for m in range(19):
            where[SLOT[m], z] = post[m]
        for s in range(2):
            for i, m in enumerate(GROUPS[1][s]):
                edge = post[m][H - 1 :, :] if s == 0 else post[m][:1, :]
                ypack[it, s, i, pl.ds(z, 1), :] = edge
        if isinstance(z, int):
            for m in ZY:
                cz, cy, _ = lattice[m]
                if z == (D - 1 if cz == 1 else 0):
                    zyline[it, m - ZY[0]] = post[m][H - 1 :, :] if cy == 1 else post[m][:1, :]
        new = []
        for s in range(2):
            acc = packs[s]
            for i, m in enumerate(GROUPS[2][s]):
                k = i * D + z
                acc = jnp.where(lane == k, pltpu.roll(post[m], k + 1 - s, 1), acc)
            new.append(acc)
        return tuple(new)

    def finish(it, packs):
        for s in range(2):
            xpack[it, s] = packs[s]

    def exchange(it):
        where = posts[it]
        moves = []
        for s in range(2):
            moves.append((xpack.at[it, s], xrecv.at[it, s], (0, 0, 1 - 2 * s)))
        for m in ZX:
            z = D - 1 if lattice[m][0] == 1 else 0
            moves.append((where.at[SLOT[m], z], zxrecv.at[it, m - ZX[0]], lattice[m]))
        for m in YX:
            s = side(lattice[m][1])
            moves.append((ypack.at[it, s, GROUPS[1][s].index(m)], yxrecv.at[it, m - YX[0]], lattice[m]))
        for m in ZY:
            moves.append((zyline.at[it, m - ZY[0]], zyrecv.at[it, m - ZY[0]], lattice[m]))
        for s in range(2):
            z = D - 1 if s == 0 else 0
            moves.append((where.at[pl.ds(5 * s, 5), z], zrecv.at[it, s], (1 - 2 * s, 0, 0)))
        for s in range(2):
            moves.append((ypack.at[it, s], yrecv.at[it, s], (0, 1 - 2 * s, 0)))
        copies = {-1: [], 0: [], 1: []}
        for i, (src, dst, offset) in enumerate(moves):
            copies[offset[0]].append(
                pltpu.make_async_remote_copy(
                    src_ref=src, dst_ref=dst, send_sem=send_sem.at[it, i],
                    recv_sem=recv_sem.at[it, i], device_id=at(offset), device_id_type=MESH))
        return copies

    def run(copies, method, incoming=False):
        conds = {1: has_down, -1: has_up} if incoming else {1: has_up, -1: has_down}
        for copy in copies.get(0, ()):
            getattr(copy, method)()
        for dz in (1, -1):
            if copies.get(dz):
                @pl.when(conds[dz])
                def _():
                    for copy in copies[dz]:
                        getattr(copy, method)()

    def cross_arrive(copies):
        run({1: copies[1], -1: copies[-1]}, "wait_recv", incoming=True)

    small[0].wait()
    zero = jnp.zeros((H, W), jnp.float32)

    def first_plane(z, packs):
        plane_in(z).wait()
        f = [pops[m, z] for m in range(19)]
        post, velocity = collide(f, solid[z] == 1)
        if isinstance(z, int) and z == D - 1:
            for d in range(3):
                speed[0, d] = velocity[d]
        return store_post(0, z, post, packs)

    packs = first_plane(0, (zero, zero))
    packs = lax.fori_loop(1, D - 1, first_plane, packs)
    packs = first_plane(D - 1, packs)
    finish(0, packs)

    up_down = jnp.where(has_up, len(cross), 0) + jnp.where(has_down, len(cross), 0)
    pl.semaphore_wait(barrier, len(flat) + up_down)

    moves0 = exchange(0)
    run({1: moves0[1], -1: moves0[-1]}, "start")
    run({0: moves0[0]}, "start")
    ends = {1: [], -1: [], 0: []}
    for s in range(2):
        dz = 1 - 2 * s
        ends[dz].append(
            pltpu.make_async_remote_copy(
                src_ref=conc, dst_ref=near.at[s], send_sem=near_sem.at[0, s],
                recv_sem=near_sem.at[1, s], device_id=at((dz, 0, 0)), device_id_type=MESH))
    run(ends, "start")

    def arrive(it, copies):
        run({0: copies[0][-2:]}, "wait_recv")

        def prepare(z, carry):
            for m in range(19):
                cz, cy, cx = lattice[m]
                v = posts[it][SLOT[m], z - cz]
                if cx:
                    v = rolled(v, cx, 1)
                if cy:
                    v = rolled(v, cy, 0)
                    if not cx:
                        s = side(cy)
                        line = yrecv[it, s, GROUPS[1][s].index(m), pl.ds(z - cz, 1), :]
                        v = jnp.where(edge_row[s], jnp.broadcast_to(line, (H, W)), v)
                pops[m, z] = v
            return carry

        lax.fori_loop(1, D - 1, prepare, 0)
        run({0: copies[0][:-2]}, "wait_recv")
        for m in YX:
            _, cy, cx = lattice[m]
            s = side(cy)
            own = rolled(yrecv[it, s, GROUPS[1][s].index(m)], cx, 1)
            far = rolled(yxrecv[it, m - YX[0]], cx, 1)
            corner[it, m - YX[0]] = jnp.where(edge_lane[side(cx)], far, own)

    def stream(it, z, place):
        where = posts[it]
        f = []
        if place == "mid":
            for m in range(19):
                cz, cy, cx = lattice[m]
                v = pops[m, z]
                if cx:
                    s = side(cx)
                    k = GROUPS[2][s].index(m) * D + z - cz
                    column = pltpu.roll(xrecv[it, s], W - k if s == 0 else W - 1 - k, 1)
                    if cy:
                        column = rolled(column, cy, 0)
                    v = jnp.where(edge_lane[s], column, v)
                    if cy:
                        line = corner[it, m - YX[0], pl.ds(z, 1), :]
                        v = jnp.where(edge_row[side(cy)], jnp.broadcast_to(line, (H, W)), v)
                f.append(v)
            return f
        for m in range(19):
            cz, cy, cx = lattice[m]
            beyond = (cz == 1 and place == "low") or (cz == -1 and place == "high")
            if beyond:
                s = side(cz)
                v = zrecv[it, s, GROUPS[0][s].index(m)]
            else:
                v = where[SLOT[m], z - cz]
            if cx:
                s = side(cx)
                if beyond:
                    column = rolled(zxrecv[it, m - ZX[0]], cx, 1)
                else:
                    k = GROUPS[2][s].index(m) * D + z - cz
                    column = pltpu.roll(xrecv[it, s], W - k if s == 0 else W - 1 - k, 1) \
                        if not (isinstance(k, int) and k == 0 and s == 0) else xrecv[it, s]
                v = jnp.where(edge_lane[s], column, rolled(v, cx, 1))
            if cy:
                s = side(cy)
                if beyond:
                    line = zyrecv[it, m - ZY[0]]
                elif cx:
                    line = corner[it, m - YX[0], pl.ds(z, 1), :]
                else:
                    line = yrecv[it, s, GROUPS[1][s].index(m), pl.ds(z - cz, 1), :]
                v = jnp.where(edge_row[s], jnp.broadcast_to(line, (H, W)), rolled(v, cy, 0))
            f.append(v)
        if place == "low":
            inflow = equilibrium_at_inlet()
            opened = ports[0] == 1
            for m in GROUPS[0][0]:
                back = where[SLOT[opposite[m]], 0]
                f[m] = jnp.where(first_mask, jnp.where(opened, inflow[m], back), f[m])
        if place == "high":
            velocity = [speed[it, d] for d in range(3)]
            outflow = balance(base_density, velocity, GROUPS[0][1])
            opened = ports[1] == 1
            for m in GROUPS[0][1]:
                back = where[SLOT[opposite[m]], D - 1]
                f[m] = jnp.where(last_mask, jnp.where(opened, outflow[m], back), f[m])
        return f

    def planes(step, carry, crossing):
        carry = lax.fori_loop(1, D - 1, lambda z, c: step(z, "mid", c), carry)
        crossing()
        carry = step(0, "low", carry)
        return step(D - 1, "high", carry)

    arrive(0, moves0)

    moves1 = exchange(1)

    def second_plane(z, place, packs):
        f = stream(0, z, place)
        post, velocity = collide(f, solid[z] == 1)
        if place == "high":
            for d in range(3):
                speed[1, d] = velocity[d]
        packs = store_post(1, z, post, packs)
        if place != "mid":
            dz = -1 if place == "low" else 1
            run({dz: moves1[dz]}, "start")
        return packs

    finish(1, planes(second_plane, (zero, zero), lambda: cross_arrive(moves0)))
    run({0: moves1[0]}, "start")

    run(ends, "wait_recv", incoming=True)
    source = lax.broadcasted_iota(jnp.int32, (ncx, ncx), 0)
    target = lax.broadcasted_iota(jnp.int32, (ncx, ncx), 1)
    ahead = jnp.where(target == ncx - 1, 0, target + 1)
    behind = jnp.where(target == 0, ncx - 1, target - 1)
    take_after = (source == ahead).astype(jnp.float32)
    take_before = (source == behind).astype(jnp.float32)

    def exact_dot(a, b):
        return jnp.dot(a, b, precision=lax.Precision.HIGHEST, preferred_element_type=jnp.float32)

    diffs = []
    for s in range(2):
        c = conc[s, 0]
        wrapped[s, 1 : ncy + 1, :] = c
        wrapped[s, 0:1, :] = conc[s, 0, ncy - 1 : ncy, :]
        wrapped[s, ncy + 1 : ncy + 2, :] = conc[s, 0, 0:1, :]
        pairs = [
            (near[0, s, 0], near[1, s, 0]),
            (wrapped[s, 0:ncy, :], wrapped[s, 2 : ncy + 2, :]),
            (exact_dot(c, take_before), exact_dot(c, take_after)),
        ]
        curvature = sum(b + a - 2.0 * c for b, a in pairs)
        rate = uptake_rate[s] * (affinity[s] * c - load[s, 0])
        new_load[s, 0] = load[s, 0] + rate
        diffs.append((c - phase_ratio * rate + spread_base[s] * curvature, curvature,
                      [(c - b, a - c) for b, a in pairs]))

    arrive(1, moves1)

    def last_plane(z, place, totals):
        f = stream(1, z, place)
        for m in range(19):
            out[m, z] = f[m]
        pore = solid[z] == 0
        return tuple(t + jnp.where(pore, flow, 0.0) for t, flow in zip(totals, momentum(f)))

    totals = planes(last_plane, (zero, zero, zero), lambda: cross_arrive(moves1))
    sums = zero
    for d in range(3):
        line = jnp.sum(totals[d], axis=0, keepdims=True)
        sums = jnp.where(row == d, jnp.broadcast_to(line, (H, W)), sums)
    wide = sent_v.shape[2]
    voxel = lax.broadcasted_iota(jnp.int32, (W, wide), 0)
    cell = lax.broadcasted_iota(jnp.int32, (W, wide), 1) - gx * (W // CELL)
    pick = ((voxel >= cell * CELL) & (voxel < cell * CELL + CELL)).astype(jnp.float32)
    mine = exact_dot(sums, pick) * (1.0 / (CELL * CELL * CELL * base_density))
    for d in range(3):
        sent_v[d] = mine[d : d + 1, :]
    tell = [
        pltpu.make_async_remote_copy(
            src_ref=sent_v, dst_ref=all_v.at[gy, gx], send_sem=vsend.at[i],
            recv_sem=vrecv.at[i], device_id=at(offset), device_id_type=MESH)
        for i, offset in enumerate(flat)
    ]
    for copy in tell:
        copy.start()
    all_v[gy, gx] = sent_v[...]
    run(moves0, "wait_send")
    run(moves1, "wait_send")
    run(ends, "wait_send")
    for copy in tell:
        copy.wait_recv()

    for y in range(ny):
        total = all_v[y, 0]
        for x in range(1, nx):
            total = total + all_v[y, x]
        for d in range(3):
            vel[d, y : y + 1, :] = total[d]
    courant = [CELL * vel[d][:, :ncx] for d in range(3)]
    reach = jnp.abs(courant[0]) + jnp.abs(courant[1]) + jnp.abs(courant[2])
    for s in range(2):
        value, curvature, steps = diffs[s]
        for d in range(3):
            low, high = steps[d]
            value = value - jnp.maximum(courant[d], 0.0) * low - jnp.minimum(courant[d], 0.0) * high
        new_conc[s, 0] = value + spread_length * reach * curvature
    for copy in tell:
        copy.wait_send()


def hand_out(*refs):
    copies = [pltpu.make_async_copy(refs[i], refs[3 + i], refs[6].at[i]) for i in range(3)]
    for copy in copies:
        copy.start()
    for copy in copies:
        copy.wait()


def equilibrium_at_inlet():
    result = {}
    for m in GROUPS[0][0]:
        along = inlet_speed
        result[m] = weights[m] * base_density * (
            1.0 + 3.0 * along + 4.5 * along * along - 1.5 * inlet_speed * inlet_speed)
    return result


def solution(mesh):
    sizes = tuple(mesh.shape[a] for a in ("gz", "gy", "gx"))
    nz, ny, nx = sizes

    def body(populations, solid, ports, concentration, loaded):
        D, H, W = solid.shape
        ncy, ncx = concentration.shape[2:]
        assert D == CELL and H == CELL and W % 128 == 0 and 5 * D <= W
        wide = -(-ncx // 128) * 128
        f32 = jnp.float32
        tile = (H, W)
        anywhere = pl.BlockSpec(memory_space=pl.ANY)
        inside = pl.BlockSpec(memory_space=pltpu.VMEM)
        results = (populations, concentration, loaded)
        made = pl.pallas_call(
            functools.partial(kernel, sizes),
            out_shape=tuple(pltpu.VMEM(a.shape, f32) for a in results),
            in_specs=[anywhere] * 5,
            out_specs=(inside,) * 3,
            scratch_shapes=[
                pltpu.VMEM(populations.shape, f32),
                pltpu.VMEM(solid.shape, jnp.int32),
                pltpu.VMEM(ports.shape, jnp.int32),
                pltpu.VMEM(concentration.shape, f32),
                pltpu.VMEM(loaded.shape, f32),
                pltpu.VMEM((19, D) + tile, f32),
                pltpu.VMEM((19, D) + tile, f32),
                pltpu.VMEM((ITERS, 3) + tile, f32),
                pltpu.VMEM((ITERS, 2, 5, D, W), f32),
                pltpu.VMEM((ITERS, 2) + tile, f32),
                pltpu.VMEM((ITERS, 4, 1, W), f32),
                pltpu.VMEM((ITERS, 2, 5) + tile, f32),
                pltpu.VMEM((ITERS, 2, 5, D, W), f32),
                pltpu.VMEM((ITERS, 2) + tile, f32),
                pltpu.VMEM((ITERS, 4, 1, W), f32),
                pltpu.VMEM((ITERS, 4) + tile, f32),
                pltpu.VMEM((ITERS, 4, D, W), f32),
                pltpu.VMEM((ITERS, 4, D, W), f32),
                pltpu.VMEM((2,) + concentration.shape, f32),
                pltpu.VMEM((2, ncy + 2, ncx), f32),
                pltpu.VMEM((3, 1, wide), f32),
                pltpu.VMEM((ny, nx, 3, 1, wide), f32),
                pltpu.VMEM((3, ncy, wide), f32),
                pltpu.SemaphoreType.DMA((D + 4,)),
                pltpu.SemaphoreType.DMA((ITERS, 18)),
                pltpu.SemaphoreType.DMA((ITERS, 18)),
                pltpu.SemaphoreType.DMA((2, 2)),
                pltpu.SemaphoreType.DMA((ny * nx - 1,)),
                pltpu.SemaphoreType.DMA((ny * nx - 1,)),
            ],
            compiler_params=pltpu.CompilerParams(collective_id=0, has_side_effects=True),
        )(populations, solid, ports, concentration, loaded)
        return pl.pallas_call(
            hand_out,
            out_shape=tuple(jax.ShapeDtypeStruct(a.shape, f32) for a in results),
            in_specs=[inside] * 3,
            out_specs=(anywhere,) * 3,
            scratch_shapes=[pltpu.SemaphoreType.DMA((3,))],
        )(*[pltpu.with_memory_space_constraint(a, pltpu.VMEM) for a in made])

    placed = (
        P(None, "gz", "gy", "gx"),
        P("gz", "gy", "gx"),
        P(None, "gy", "gx"),
        P(None, "gz", None, None),
        P(None, "gz", None, None),
    )
    return jax.shard_map(
        body,
        mesh=mesh,
        in_specs=placed,
        out_specs=(P(None, "gz", "gy", "gx"), P(None, "gz", None, None), P(None, "gz", None, None)),
        check_vma=False,
    )
```
